32 devices in a mesh: ctx: 4 (over y, x), exp: 8 (over z, core).
Axes of the slice: x: 2, y: 2, z: 4, core: 2. Of those that a mesh axis runs over, the one named last changes fastest.
Arguments:
- residual: bfloat16 [512, 4096], P('ctx'), may hold values from -4 to 4
- ssm_input: bfloat16 [512, 8192], P('ctx', 'exp'), may hold values from -16 to 16
- ssm_gate: bfloat16 [512, 8192], P('ctx', 'exp'), may hold values from -5 to 5
- write_vectors: bfloat16 [512, 128], P('ctx'), may hold values from -1.75 to 1.75
- read_vectors: bfloat16 [512, 128], P('ctx'), may hold values from -1.75 to 1.75
- step_logits: float32 [128, 512], P('exp', 'ctx'), may hold values from -2 to 1536
- decay_log: float32 [128], P('exp'), may hold values from -12 to -2
- skip_gain: float32 [128], P('exp'), may hold values from 0.5 to 3
- norm_gain: float32 [8192], P('exp'), may hold values from 0.1 to 1.9
- out_weight: bfloat16 [8192, 4096], P('exp', 'ctx'), may hold values from -0.09375 to 0.09375
- moe_gain: float32 [4096], replicated, may hold values from 0.1 to 1.9
- gate_weight: bfloat16 [8, 4096, 12288], P('exp', None, 'ctx'), may hold values from -0.09375 to 0.09375
- up_weight: bfloat16 [8, 4096, 12288], P('exp', None, 'ctx'), may hold values from -0.09375 to 0.09375
- down_weight: bfloat16 [8, 12288, 4096], P('exp', 'ctx'), may hold values from -0.0546875 to 0.0546875
- expert_ids: int32 [512, 2], P('ctx'), may hold values from 0 to 7, all different within a row; in each aligned block of 128 rows (0 to 127, 128 to 255, ...) at most 64 rows name the same one
- route_weight: float32 [512, 2], P('ctx'), may hold values from 0.5 to 1.5
Outputs:
- layer_out: bfloat16 [512, 4096], P('ctx', 'exp')
The draws below stay inside these ranges and needn't reach their ends.
Inputs may be any that keep to these rules, and one draw needn't show every extreme that they name: `expert_ids`: each row names 2 different experts. Among the 128 rows of one index of ctx no expert is named by more than 64 rows, and in every draw some expert is named by exactly 64 of them.
All inputs are finite; a program needn't handle non-finite values.
Results may differ from the reference program's by a relative error of at most 0.023.
Values may be sent and summed in bfloat16 or wider, within the bound.
A program may use at most 192 MiB of HBM per device.

```python
import math
import jax
import jax.numpy as jnp
import numpy as np
from jax import lax

D = 4096
SSM_HEADS = 128
HEAD_DIM = 64
STATE = 128
SPAN = 128
NORM_GROUP = 512
EXPERTS = 8
FF = 12288
TOP = 2
TOK_CTX = 128
WINDOW_TOKENS = 512
INNER = 8192
PIECES = 8
FF_PART = 12288
CAP = 64
N_CTX = 4
N_EXP = 8


def spike_positions(key):
    return jax.random.randint(jax.random.fold_in(key, 29), (2,), 0, WINDOW_TOKENS)


def spike_token_rows(key):
    token_positions = spike_positions(key)
    return jnp.any(jnp.arange(WINDOW_TOKENS)[:, None] == token_positions[None, :], axis=1)


def scaled_field(key, row_count, col_count):
    key_rows, key_cols, key_vals = jax.random.split(key, 3)
    row_scale = 10.0 ** jax.random.uniform(key_rows, (row_count, 1), jnp.float32, -0.5, 0.5)
    col_scale = 10.0 ** jax.random.uniform(key_cols, (1, col_count), jnp.float32, -0.5, 0.5)
    values = 0.5 * jnp.clip(jax.random.normal(key_vals, (row_count, col_count), jnp.float32), -3.0, 3.0)
    return values * row_scale * col_scale


def decay_plan(key):
    key_kind, key_slow, key_fast = jax.random.split(jax.random.fold_in(key, 17), 3)
    slow_share = 0.5
    slow_head_mask = jax.random.uniform(key_kind, (SSM_HEADS,), jnp.float32) < slow_share
    slow_rate = jax.random.uniform(key_slow, (SSM_HEADS,), jnp.float32, 0.2, 0.9) / WINDOW_TOKENS
    fast_rate = 1.0 / jax.random.uniform(key_fast, (SSM_HEADS,), jnp.float32, 20.0, 40.0)
    return (jnp.where(slow_head_mask, slow_rate, fast_rate), slow_head_mask)


def draw_residual(key, part):
    return (0.25 * scaled_field(jax.random.fold_in(key, 3), WINDOW_TOKENS, D)).astype(jnp.bfloat16)


def draw_ssm_input(key, part):
    signal_field_values = scaled_field(jax.random.fold_in(key, 5), WINDOW_TOKENS, INNER)
    token_at_spike = spike_token_rows(key)
    return jnp.where(token_at_spike[:, None], signal_field_values / WINDOW_TOKENS, signal_field_values).astype(jnp.bfloat16)


def draw_decay_log(key, part):
    decay_rate_by_head = decay_plan(key)[0]
    return jnp.log(decay_rate_by_head).astype(jnp.float32)


def draw_step_logits(key, part):
    decay_rate_by_head, slow_head_mask = decay_plan(key)
    key_base, key_phase, key_loss = jax.random.split(jax.random.fold_in(key, 23), 3)
    base_step = 10.0 ** jax.random.uniform(key_base, (SSM_HEADS, WINDOW_TOKENS), jnp.float32, -0.4, 0.2)
    phase_shift = jax.random.uniform(key_phase, (SSM_HEADS, 1), jnp.float32, 0.0, 1.0)
    position_ramp = jnp.arange(WINDOW_TOKENS, dtype=jnp.float32)[None, :] / WINDOW_TOKENS
    wave_factor = jnp.exp(0.6 * jnp.sin(6.283185307 * (position_ramp + phase_shift)))
    steady_level = base_step * wave_factor
    balance_loss_share = jax.random.uniform(key_loss, (SSM_HEADS, 1), jnp.float32, 0.22, 0.51)
    spike_step_size = jnp.where(slow_head_mask[:, None], balance_loss_share / decay_rate_by_head[:, None], 3.0)
    token_at_spike = spike_token_rows(key)
    step_size_value = jnp.where(token_at_spike[None, :], spike_step_size, steady_level)
    return (step_size_value + jnp.log(-jnp.expm1(-step_size_value))).astype(jnp.float32)


def raised(result, rng, source, target, blocks, factor):
    def block_of(position):
        return (jnp.arange(result.shape[position]) // (result.shape[position] // blocks)).reshape((-1,) + (1,) * (result.ndim - 1 - position))

    first = jax.random.permutation(rng, blocks)[block_of(target)]
    far = (block_of(target) + blocks // 2) % blocks
    return jnp.where((block_of(source) == first) | (block_of(source) == far), factor * result, result)


def level_of(key, dims, cuts, smallest, high):
    gain = 1.0
    for axis_at, parts in cuts:
        steps = jax.random.uniform(jax.random.fold_in(jax.random.fold_in(key, 6), axis_at), (parts,), jnp.float32, smallest / len(cuts), high / len(cuts))
        gain = gain * jnp.repeat(jnp.exp(steps), dims[axis_at] // parts).reshape((-1,) + (1,) * (len(dims) - 1 - axis_at))
    return gain


def assign_block(own_key, own, number, rows, count, top, limit, slope):
    order = jax.random.permutation(own_key, count)
    packed, usual = portions_of(count, rows * top, limit, slope, True), portions_of(count, rows * top, limit, slope, False)
    places = jnp.arange(count)

    def named(sizes, offset_by):
        used = int((sizes > 0).sum())
        fixed = max(1, used // 4)
        passed = fixed + (places - fixed + offset_by * (used - fixed)) % max(1, count - fixed)
        return jnp.zeros((count,), jnp.int32).at[order[jnp.where(places < fixed, places, passed)]].set(jnp.asarray(sizes, jnp.int32))

    sizes = jnp.where(number % 4 == 0, named(packed, number // 4), named(usual, number - number // 4 - 1))
    mixed = jax.random.permutation(jax.random.fold_in(own, 3), count)
    source_of, taker = mixed[0:count // 2 * 2:2], mixed[1:count // 2 * 2:2]
    slack = jnp.minimum(sizes[source_of] - 1, limit - sizes[taker]) // 2
    slack = jnp.where((source_of == order[0]) | (taker == order[0]) | (sizes[taker] == 0), 0, jnp.maximum(slack, 0))
    passed = jax.random.randint(jax.random.fold_in(own, 4), (count // 2,), 0, 1 << 20) % (slack + 1)
    sizes = sizes.at[source_of].add(-passed).at[taker].add(passed)
    members = jnp.searchsorted(jnp.cumsum(sizes), jnp.arange(rows * top), side="right").astype(jnp.int32)
    grid = members.reshape(top, rows).T
    grid = grid[jax.random.permutation(jax.random.fold_in(own, 1), rows)]
    offset_by = jax.random.randint(jax.random.fold_in(own, 2), (rows, 1), 0, top)
    return jnp.take_along_axis(grid, (jnp.arange(top)[None, :] + offset_by) % top, axis=1)


def portions_of(number_of, total, reach, slope, full):
    loads = [(1 << 20) // math.isqrt(grade ** slope) + 1 for grade in range(1, number_of + 1)]
    largest = reach if full else min(reach, max(-(-total // number_of), total * loads[0] // sum(loads)))
    least = 1 if total - largest >= number_of - 1 else 0
    counts, spare = [largest] + [least] * (number_of - 1), total - largest - least * (number_of - 1)
    while spare > 0:
        free = [i for i in range(1, number_of) if counts[i] < largest] or [i for i in range(1, number_of) if counts[i] < reach]
        pool, remaining = sum([loads[i] for i in free]), spare
        for i in free:
            extra = min(reach - counts[i], max(1, remaining * loads[i] // pool), spare)
            counts[i] = counts[i] + extra
            spare = spare - extra
    return np.array(counts)


def centred(key, dims, scale, most, cuts=(), kind=jnp.bfloat16):
    entries = jax.random.normal(key, dims, jnp.float32) * scale
    if len(cuts) > 0:
        entries = level_of(key, dims, cuts, -0.22, 0.18) * entries
    return jnp.clip(entries, min=-most, max=most).astype(kind)


def gaussian_with(key, extent, spread, bound, pieces, heavy, kind=jnp.bfloat16):
    array = spread * jax.random.normal(key, extent, jnp.float32)
    if pieces:
        array = array * level_of(key, extent, pieces, -0.22, 0.18)
    return jnp.clip(raised(array, jax.random.fold_in(key, 3), *heavy), -bound, bound).astype(kind)


def setup_inputs(seed: int = 0) -> dict:
    arg_keys = jax.random.split(jax.random.key(seed), 17)
    residual = draw_residual(jax.random.fold_in(arg_keys[16], 71), 0)
    ssm_input = draw_ssm_input(jax.random.fold_in(arg_keys[16], 71), 0)
    ssm_gate = centred(arg_keys[2], (WINDOW_TOKENS, INNER), 1.0, 5.0, ((0, 4), (1, 8)))
    write_vectors = centred(arg_keys[3], (WINDOW_TOKENS, STATE), 0.3, 1.75, ((0, 4),))
    read_vectors = centred(arg_keys[4], (WINDOW_TOKENS, STATE), 0.3, 1.75, ((0, 4),))
    step_logits = draw_step_logits(jax.random.fold_in(arg_keys[16], 71), 0)
    decay_log = draw_decay_log(jax.random.fold_in(arg_keys[16], 71), 0)
    skip_gain = jnp.clip(0.5 + 2.5 * jax.random.uniform(arg_keys[7], (SSM_HEADS,), jnp.float32) ** level_of(arg_keys[7], (SSM_HEADS,), ((0, 8),), -0.2, 0.2), 0.5, 3.0)
    norm_gain = jnp.clip(1.0 + 0.18 * jax.random.normal(arg_keys[8], (INNER,), jnp.float32), 0.1, 1.9)
    out_weight = gaussian_with(arg_keys[9], (INNER, D), INNER ** -0.5, 0.09375, ((0, 8), (1, 4)), (0, 1, 8, 2.0))
    moe_gain = jnp.clip(1.0 + 0.18 * jax.random.normal(arg_keys[10], (D,), jnp.float32), 0.1, 1.9)
    gate_weight = centred(arg_keys[11], (PIECES, D, FF_PART), D ** -0.5, 0.09375, ((0, 8), (2, 4)))
    up_weight = centred(arg_keys[12], (PIECES, D, FF_PART), D ** -0.5, 0.09375, ((0, 8), (2, 4)))
    down_weight = centred(arg_keys[13], (PIECES, FF_PART, D), FF ** -0.5, 0.0546875, ((0, 8), (1, 4)))
    expert_ids_keys = jax.random.split(jax.random.fold_in(arg_keys[14], 1), WINDOW_TOKENS // TOK_CTX)
    expert_ids_turns = jax.random.permutation(jax.random.fold_in(arg_keys[14], 3), WINDOW_TOKENS // TOK_CTX)
    expert_ids = jax.vmap(lambda own, number: assign_block(jax.random.fold_in(arg_keys[14], 2), own, number, TOK_CTX, EXPERTS, TOP, CAP, 2))(expert_ids_keys, expert_ids_turns).reshape((WINDOW_TOKENS, TOP))
    route_weight = jnp.clip(0.5 + 1.0 * jax.random.uniform(arg_keys[15], (WINDOW_TOKENS, TOP), jnp.float32) ** level_of(arg_keys[15], (WINDOW_TOKENS, TOP), ((0, 4),), -0.2, 0.2), 0.5, 1.5)
    return {"residual": residual, "ssm_input": ssm_input, "ssm_gate": ssm_gate, "write_vectors": write_vectors, "read_vectors": read_vectors, "step_logits": step_logits, "decay_log": decay_log, "skip_gain": skip_gain, "norm_gain": norm_gain, "out_weight": out_weight, "moe_gain": moe_gain, "gate_weight": gate_weight, "up_weight": up_weight, "down_weight": down_weight, "expert_ids": expert_ids, "route_weight": route_weight}


EPSILON = 1e-05

def slot_tables(block_ids):
    expert_range = jnp.arange(EXPERTS, dtype=jnp.int32)
    hit_table = lax.optimization_barrier(jnp.sum((block_ids[:, :, None] == expert_range[None, None, :]).astype(jnp.int32), axis=1))
    ranking = jnp.cumsum(hit_table, axis=0).astype(jnp.int32) - 1
    slot_range = jnp.arange(CAP, dtype=jnp.int32)
    matches = (hit_table.T[:, None, :] == 1) & (ranking.T[:, None, :] == slot_range[None, :, None])
    row_count = block_ids.shape[0]
    row_range = jnp.arange(row_count, dtype=jnp.int32)
    chosen = lax.optimization_barrier(jnp.sum(jnp.where(matches, row_range[None, None, :], 0), axis=2)).astype(jnp.int32)
    filled = jnp.any(matches, axis=2)
    token_of_slot = jnp.where(filled, chosen, row_count).astype(jnp.int32)
    pick_rank = jnp.take_along_axis(ranking, block_ids, axis=1).astype(jnp.int32)
    return (token_of_slot, pick_rank)

def head_scan(cumulative, step_blocks, input_blocks, scores, write_blocks, read_wide, skip_value):
    causal = jnp.arange(SPAN)[:, None] >= jnp.arange(SPAN)[None, :]
    log_gaps = cumulative[:, :, None] - cumulative[:, None, :]
    mixing = jnp.where(causal[None], scores * jnp.exp(jnp.where(causal[None], log_gaps, 0.0)) * step_blocks[:, None, :], 0.0).astype(jnp.bfloat16)
    input_wide = input_blocks.astype(jnp.float32)
    intra_out = jnp.einsum('kts,ksp->ktp', mixing.astype(jnp.float32), input_wide, precision=lax.Precision.HIGHEST)
    end_weight = jnp.exp(cumulative[:, -1:] - cumulative) * step_blocks
    loaded = (end_weight[:, :, None] * write_blocks.astype(jnp.float32)).astype(jnp.bfloat16)
    block_state = jnp.einsum('ksp,ksn->kpn', input_wide, loaded.astype(jnp.float32), precision=lax.Precision.HIGHEST)
    block_decay = jnp.exp(cumulative[:, -1])

    def advance(carried, inputs):
        decay_now, state_now = inputs
        return (decay_now * carried + state_now, carried)
    zero_state = jnp.zeros(block_state.shape[1:], jnp.float32)
    entering = lax.scan(advance, zero_state, (block_decay, block_state))[1]
    inter_out = jnp.exp(cumulative)[:, :, None] * jnp.einsum('ktn,kpn->ktp', read_wide, entering, precision=lax.Precision.HIGHEST)
    return intra_out + inter_out + skip_value * input_wide

def reference(residual, ssm_input, ssm_gate, write_vectors, read_vectors, step_logits, decay_log, skip_gain, norm_gain, out_weight, moe_gain, gate_weight, up_weight, down_weight, expert_ids, route_weight):
    span_count = WINDOW_TOKENS // SPAN
    step_size = jax.nn.softplus(step_logits)
    log_step = step_size * (-jnp.exp(decay_log))[:, None]
    cumulative = jnp.cumsum(log_step.reshape(SSM_HEADS, span_count, SPAN), axis=2)
    step_blocks = step_size.reshape(SSM_HEADS, span_count, SPAN)
    input_heads = jnp.transpose(ssm_input.reshape(span_count, SPAN, SSM_HEADS, HEAD_DIM), (2, 0, 1, 3))
    write_blocks = write_vectors.reshape(span_count, SPAN, STATE)
    read_wide = read_vectors.reshape(span_count, SPAN, STATE).astype(jnp.float32)
    scores = jnp.einsum('ktn,ksn->kts', read_wide, write_blocks.astype(jnp.float32), precision=lax.Precision.HIGHEST)

    def per_head(items):
        return head_scan(items[0], items[1], items[2], scores, write_blocks, read_wide, items[3])
    head_outs = lax.map(per_head, (cumulative, step_blocks, input_heads, skip_gain))
    scan_out = jnp.transpose(head_outs, (1, 2, 0, 3)).reshape(WINDOW_TOKENS, INNER)
    gated_out = scan_out * jax.nn.silu(ssm_gate.astype(jnp.float32))
    grouped = gated_out.reshape(WINDOW_TOKENS, INNER // NORM_GROUP, NORM_GROUP)
    scale_inv = lax.rsqrt(lax.optimization_barrier(jnp.mean(grouped * grouped, axis=2, keepdims=True)) + EPSILON)
    normed = ((grouped * scale_inv).reshape(WINDOW_TOKENS, INNER) * norm_gain).astype(jnp.bfloat16)
    ssm_out = jnp.dot(normed, out_weight, preferred_element_type=jnp.float32)
    stream = (residual.astype(jnp.float32) + ssm_out).astype(jnp.bfloat16)
    stream_wide = stream.astype(jnp.float32)
    moe_scale = lax.rsqrt(lax.optimization_barrier(jnp.mean(stream_wide * stream_wide, axis=1, keepdims=True)) + EPSILON)
    moe_in = (stream_wide * moe_scale * moe_gain).astype(jnp.bfloat16)
    split_count = N_EXP // EXPERTS
    piece_width = FF_PART // N_CTX
    token_of_slot, pick_rank = jax.vmap(slot_tables)(expert_ids.reshape(N_CTX, TOK_CTX, TOP))
    padded = jnp.concatenate([moe_in.reshape(N_CTX, TOK_CTX, D), jnp.zeros((N_CTX, 1, D), jnp.bfloat16)], axis=1)
    gathered = jax.vmap(lambda table_rows, slot_index: jnp.take(table_rows, slot_index, axis=0))(padded, token_of_slot)
    expert_rows = jnp.transpose(gathered, (1, 0, 2, 3)).reshape(EXPERTS, N_CTX * CAP, D)

    def piece_out(piece_index):
        piece_rows = lax.dynamic_index_in_dim(expert_rows, piece_index // split_count, 0, keepdims=False).astype(jnp.float32)
        gate_piece = lax.dynamic_index_in_dim(gate_weight, piece_index, 0, keepdims=False)
        up_piece = lax.dynamic_index_in_dim(up_weight, piece_index, 0, keepdims=False)
        down_piece = lax.dynamic_index_in_dim(down_weight, piece_index, 0, keepdims=False)

        def add_block(total, ctx_index):
            first_col = (ctx_index * piece_width).astype(jnp.int32)
            gate_cols = lax.dynamic_slice_in_dim(gate_piece, first_col, piece_width, 1).astype(jnp.float32)
            up_cols = lax.dynamic_slice_in_dim(up_piece, first_col, piece_width, 1).astype(jnp.float32)
            down_rows = lax.dynamic_slice_in_dim(down_piece, first_col, piece_width, 0).astype(jnp.float32)
            gate_val = jnp.dot(piece_rows, gate_cols, precision=lax.Precision.HIGHEST, preferred_element_type=jnp.float32)
            up_val = jnp.dot(piece_rows, up_cols, precision=lax.Precision.HIGHEST, preferred_element_type=jnp.float32)
            hidden = (jax.nn.silu(gate_val) * up_val).astype(jnp.bfloat16)
            piece_term = jnp.dot(hidden.astype(jnp.float32), down_rows, precision=lax.Precision.HIGHEST, preferred_element_type=jnp.float32)
            piece_term = lax.optimization_barrier(piece_term.astype(jnp.bfloat16)).astype(jnp.float32)
            return (total + piece_term, None)
        return lax.scan(add_block, jnp.zeros((N_CTX * CAP, D), jnp.float32), jnp.arange(N_CTX, dtype=jnp.int32))[0]
    pieces_out = lax.map(piece_out, jnp.arange(N_EXP, dtype=jnp.int32))
    block_of = jnp.arange(WINDOW_TOKENS, dtype=jnp.int32) // TOK_CTX
    row_index = (block_of[:, None] * CAP + pick_rank.reshape(WINDOW_TOKENS, TOP)).astype(jnp.int32)
    piece_index = (expert_ids[:, :, None] * split_count + jnp.arange(split_count, dtype=jnp.int32)[None, None, :]).astype(jnp.int32)
    picked = pieces_out[piece_index, row_index[:, :, None]]
    moe_out = lax.optimization_barrier(jnp.sum(route_weight[:, :, None] * lax.optimization_barrier(jnp.sum(picked, axis=2)), axis=1))
    return (stream_wide + moe_out).astype(jnp.bfloat16)
```

```python
import functools
import math

import jax
import jax.numpy as jnp
from jax import lax
from jax.experimental import pallas as pl
from jax.experimental.pallas import tpu as pltpu
from jax.sharding import PartitionSpec as P

SPAN = 128
NORM_GROUP = 512
EXPERTS = 8
CAP = 64


EPSILON = 1e-05


MESH = pl.DeviceIdType.MESH


def send_kernel(axis, count, pair, spread, n_arrays, *refs):
    sources, targets = refs[:n_arrays], refs[n_arrays : 2 * n_arrays]
    local_sem, send_sem, recv_sem = refs[2 * n_arrays :]
    index = lax.axis_index(axis)
    group, lane = index // pair, lax.rem(index, pair)
    barrier = pltpu.get_barrier_semaphore()
    peers = [lax.rem(group + d, count) for d in range(1, count)]
    for peer in peers:
        pl.semaphore_signal(
            barrier, inc=1, device_id={axis: peer * pair + lane}, device_id_type=MESH
        )
    pl.semaphore_wait(barrier, count - 1)
    copies = []
    for d, peer in enumerate(peers):
        for i in range(n_arrays):
            copy = pltpu.make_async_remote_copy(
                src_ref=sources[i] if spread else sources[i].at[peer],
                dst_ref=targets[i].at[group],
                send_sem=send_sem.at[d, i],
                recv_sem=recv_sem.at[d, i],
                device_id={axis: peer * pair + lane},
                device_id_type=MESH,
            )
            copy.start()
            copies.append(copy)
    for i in range(n_arrays):
        own = pltpu.make_async_copy(
            sources[i] if spread else sources[i].at[group],
            targets[i].at[group],
            local_sem.at[i],
        )
        own.start()
        copies.append(own)
    for copy in copies:
        copy.wait()


def sent(arrays, axis, number, spread, pair=1):
    count = lax.axis_size(axis) // pair
    n_arrays = len(arrays)
    shapes = [
        jax.ShapeDtypeStruct((count,) + a.shape if spread else a.shape, a.dtype) for a in arrays
    ]
    size = sum(math.prod(shape.shape) * shape.dtype.itemsize for shape in shapes)
    return pl.pallas_call(
        functools.partial(send_kernel, axis, count, pair, spread, n_arrays),
        out_shape=shapes,
        in_specs=[pl.BlockSpec(memory_space=pl.ANY)] * n_arrays,
        out_specs=[pl.BlockSpec(memory_space=pl.ANY)] * n_arrays,
        scratch_shapes=[
            pltpu.SemaphoreType.DMA((n_arrays,)),
            pltpu.SemaphoreType.DMA((count - 1, n_arrays)),
            pltpu.SemaphoreType.DMA((count - 1, n_arrays)),
        ],
        compiler_params=pltpu.CompilerParams(collective_id=number, has_side_effects=True),
        cost_estimate=pl.CostEstimate(flops=0, bytes_accessed=2 * size, transcendentals=0),
    )(*arrays)


def gather_pairs_kernel(axis, groups, x_ref, out_ref, local_sem, send_sem, recv_sem, pass_send, pass_recv):
    index = lax.axis_index(axis)
    group, lane = index // 2, lax.rem(index, 2)
    sibling = group * 2 + 1 - lane
    barrier = pltpu.get_barrier_semaphore()
    peers = [lax.rem(group + d, groups) for d in range(1, groups)]
    for peer in [p * 2 + lane for p in peers] + [sibling]:
        pl.semaphore_signal(barrier, inc=1, device_id={axis: peer}, device_id_type=MESH)
    pl.semaphore_wait(barrier, groups)
    copies = []
    for d, peer in enumerate(peers):
        copy = pltpu.make_async_remote_copy(
            src_ref=x_ref,
            dst_ref=out_ref.at[index],
            send_sem=send_sem.at[d],
            recv_sem=recv_sem.at[d],
            device_id={axis: peer * 2 + lane},
            device_id_type=MESH,
        )
        copy.start()
        copies.append(copy)
    own = pltpu.make_async_copy(x_ref, out_ref.at[index], local_sem)
    own.start()
    passed = [
        pltpu.make_async_remote_copy(
            src_ref=x_ref,
            dst_ref=out_ref.at[index],
            send_sem=pass_send.at[0],
            recv_sem=pass_recv.at[0],
            device_id={axis: sibling},
            device_id_type=MESH,
        )
    ]
    passed[0].start()
    for d in range(1, groups):
        copies[d - 1].wait_recv()
        block = lax.rem(group + groups - d, groups) * 2 + lane
        copy = pltpu.make_async_remote_copy(
            src_ref=out_ref.at[block],
            dst_ref=out_ref.at[block],
            send_sem=pass_send.at[d],
            recv_sem=pass_recv.at[d],
            device_id={axis: sibling},
            device_id_type=MESH,
        )
        copy.start()
        passed.append(copy)
    for copy in copies:
        copy.wait_send()
    own.wait()
    for copy in passed:
        copy.wait()


def gather_pairs(x, axis, number):
    count = lax.axis_size(axis)
    return pl.pallas_call(
        functools.partial(gather_pairs_kernel, axis, count // 2),
        out_shape=jax.ShapeDtypeStruct((count,) + x.shape, x.dtype),
        in_specs=[pl.BlockSpec(memory_space=pl.ANY)],
        out_specs=pl.BlockSpec(memory_space=pl.ANY),
        scratch_shapes=[
            pltpu.SemaphoreType.DMA,
            pltpu.SemaphoreType.DMA((count // 2 - 1,)),
            pltpu.SemaphoreType.DMA((count // 2 - 1,)),
            pltpu.SemaphoreType.DMA((count // 2,)),
            pltpu.SemaphoreType.DMA((count // 2,)),
        ],
        compiler_params=pltpu.CompilerParams(collective_id=number, has_side_effects=True),
        cost_estimate=pl.CostEstimate(
            flops=0, bytes_accessed=2 * count * x.size * x.dtype.itemsize, transcendentals=0
        ),
    )(x)


def pair_sum(halves, number):
    lane = lax.rem(lax.axis_index("exp"), 2)
    both = pair_send(halves, number)
    own = lax.dynamic_index_in_dim(halves, lane, 0, keepdims=False)
    return (own.astype(jnp.float32) + both.astype(jnp.float32)).astype(jnp.bfloat16)


def pair_kernel(x_ref, out_ref, send_sem, recv_sem):
    index = lax.axis_index("exp")
    lane = lax.rem(index, 2)
    sibling = index + 1 - 2 * lane
    barrier = pltpu.get_barrier_semaphore()
    pl.semaphore_signal(barrier, inc=1, device_id={"exp": sibling}, device_id_type=MESH)
    pl.semaphore_wait(barrier, 1)
    copy = pltpu.make_async_remote_copy(
        src_ref=x_ref.at[1 - lane],
        dst_ref=out_ref,
        send_sem=send_sem,
        recv_sem=recv_sem,
        device_id={"exp": sibling},
        device_id_type=MESH,
    )
    copy.start()
    copy.wait()


def pair_send(halves, number):
    return pl.pallas_call(
        pair_kernel,
        out_shape=jax.ShapeDtypeStruct(halves.shape[1:], halves.dtype),
        in_specs=[pl.BlockSpec(memory_space=pl.ANY)],
        out_specs=pl.BlockSpec(memory_space=pl.ANY),
        scratch_shapes=[pltpu.SemaphoreType.DMA, pltpu.SemaphoreType.DMA],
        compiler_params=pltpu.CompilerParams(collective_id=number, has_side_effects=True),
        cost_estimate=pl.CostEstimate(
            flops=0, bytes_accessed=halves.size * 2, transcendentals=0
        ),
    )(halves)


def slot_tables(block_ids):
    expert_range = jnp.arange(EXPERTS, dtype=jnp.int32)
    hit_table = jnp.sum(
        (block_ids[:, :, None] == expert_range[None, None, :]).astype(jnp.int32), axis=1
    )
    ranking = jnp.cumsum(hit_table, axis=0) - 1
    slot_range = jnp.arange(CAP, dtype=jnp.int32)
    matches = (hit_table.T[:, None, :] == 1) & (ranking.T[:, None, :] == slot_range[None, :, None])
    row_count = block_ids.shape[0]
    row_range = jnp.arange(row_count, dtype=jnp.int32)
    chosen = jnp.sum(jnp.where(matches, row_range[None, None, :], 0), axis=2)
    filled = jnp.any(matches, axis=2)
    token_of_slot = jnp.where(filled, chosen, row_count)
    pick_rank = jnp.take_along_axis(ranking, block_ids, axis=1)
    return (token_of_slot, pick_rank)


def normalize(stream_rows, moe_gain):
    values = stream_rows.astype(jnp.float32)
    scale_inv = lax.rsqrt(jnp.mean(values * values, axis=-1, keepdims=True) + EPSILON)
    return (values * scale_inv * moe_gain).astype(jnp.bfloat16)


def body(
    residual,
    ssm_input,
    ssm_gate,
    write_vectors,
    read_vectors,
    step_logits,
    decay_log,
    skip_gain,
    norm_gain,
    out_weight,
    moe_gain,
    gate_weight,
    up_weight,
    down_weight,
    expert_ids,
    route_weight,
):
    heads_dev = step_logits.shape[0]
    tok_rows = step_logits.shape[1]
    head_width = ssm_input.shape[1] // heads_dev
    span_count = tok_rows // SPAN
    step_size = jax.nn.softplus(step_logits)
    log_step = step_size * (-jnp.exp(decay_log))[:, None]
    cumulative = jnp.cumsum(log_step.reshape(heads_dev, span_count, SPAN), axis=2)
    step_blocks = step_size.reshape(heads_dev, span_count, SPAN)
    input_blocks = ssm_input.reshape(span_count, SPAN, heads_dev, head_width)
    write_blocks = write_vectors.reshape(span_count, SPAN, -1)
    read_blocks = read_vectors.reshape(span_count, SPAN, -1)
    scores = jnp.einsum(
        "ktn,ksn->kts", read_blocks, write_blocks, preferred_element_type=jnp.float32
    )
    causal = jnp.arange(SPAN)[:, None] >= jnp.arange(SPAN)[None, :]
    log_gaps = cumulative[:, :, :, None] - cumulative[:, :, None, :]
    mixing = jnp.where(
        causal,
        scores[None] * jnp.exp(jnp.where(causal, log_gaps, 0.0)) * step_blocks[:, :, None, :],
        0.0,
    ).astype(jnp.bfloat16)
    intra_out = jnp.einsum(
        "hkts,kshp->kthp", mixing, input_blocks, preferred_element_type=jnp.float32
    )
    end_weight = jnp.exp(cumulative[:, :, -1:] - cumulative) * step_blocks
    loaded = (end_weight[:, :, :, None] * write_blocks.astype(jnp.float32)[None]).astype(
        jnp.bfloat16
    )
    block_state = jnp.einsum(
        "kshp,hksn->hkpn", input_blocks, loaded, preferred_element_type=jnp.float32
    )
    block_decay = jnp.exp(cumulative[:, :, -1])
    running = jnp.zeros_like(block_state[:, 0])
    decay_run = jnp.ones_like(block_decay[:, 0])
    entering_list = [running]
    reach_list = [decay_run]
    running = block_decay[:, 0, None, None] * running + block_state[:, 0]
    decay_run = decay_run * block_decay[:, 0]
    device_state = running
    device_decay = decay_run

    all_states, all_decays = sent(
        [
            device_state.astype(jnp.bfloat16),
            jnp.broadcast_to(device_decay[:, None], (heads_dev, 128)),
        ],
        "ctx",
        1,
        True,
    )
    ctx_index = lax.axis_index("ctx")
    device_in = jnp.zeros_like(device_state)
    for j in range(lax.axis_size("ctx") - 1):
        device_in = jnp.where(
            j < ctx_index,
            all_decays[j, :, :1, None] * device_in + all_states[j].astype(jnp.float32),
            device_in,
        )
    entering = jnp.stack(entering_list, axis=1)
    reach = jnp.stack(reach_list, axis=1)
    states = entering + reach[:, :, None, None] * device_in[:, None]
    inter_out = jnp.transpose(jnp.exp(cumulative), (1, 2, 0))[:, :, :, None] * jnp.einsum(
        "ktn,hkpn->kthp", read_blocks.astype(jnp.float32), states, precision=lax.Precision.HIGHEST
    )
    scan_out = (
        intra_out + inter_out + skip_gain[None, None, :, None] * input_blocks.astype(jnp.float32)
    )
    scan_out = scan_out.reshape(tok_rows, heads_dev * head_width)
    gated_out = scan_out * jax.nn.silu(ssm_gate.astype(jnp.float32))
    grouped = gated_out.reshape(tok_rows, -1, NORM_GROUP)
    group_scale = lax.rsqrt(jnp.mean(grouped * grouped, axis=2, keepdims=True) + EPSILON)
    normed = ((grouped * group_scale).reshape(tok_rows, -1) * norm_gain).astype(jnp.bfloat16)
    ctx_count = lax.axis_size("ctx")
    exp_count = lax.axis_size("exp")
    exp_index = lax.axis_index("exp")
    width = residual.shape[1]
    slice_width = width // exp_count
    split_count = exp_count // EXPERTS
    own_rows = tok_rows // exp_count
    normed_all = sent([normed], "ctx", 2, True)[0].reshape(ctx_count * tok_rows, -1)
    ssm_terms = jnp.dot(normed_all, out_weight, preferred_element_type=jnp.float32).astype(
        jnp.bfloat16
    )
    groups = exp_count // 2
    by_owner = jnp.transpose(
        ssm_terms.reshape(ctx_count, groups, 2, own_rows, -1), (2, 1, 0, 3, 4)
    ).reshape(2, groups * ctx_count * own_rows, -1)
    halves = pair_sum(by_owner, 3)
    chips = sent([halves.reshape(groups, ctx_count * own_rows, -1)], "exp", 4, False, 2)[0]
    ssm_part = jnp.sum(chips.astype(jnp.float32), axis=0).astype(jnp.bfloat16)
    ssm_rows = sent([ssm_part.reshape(ctx_count, own_rows, -1)], "ctx", 5, False)[0]
    ssm_rows = jnp.transpose(ssm_rows, (1, 0, 2)).reshape(own_rows, width)
    own_residual = lax.dynamic_slice_in_dim(residual, exp_index * own_rows, own_rows, 0)
    stream_rows = (own_residual.astype(jnp.float32) + ssm_rows.astype(jnp.float32)).astype(
        jnp.bfloat16
    )
    token_of_slot, pick_rank = slot_tables(expert_ids)
    stream_full = gather_pairs(stream_rows, "exp", 6).reshape(tok_rows, width)
    stream_slice = lax.dynamic_slice_in_dim(stream_full, exp_index * slice_width, slice_width, 1)
    padded = jnp.concatenate(
        [stream_full, jnp.zeros((1, stream_full.shape[1]), jnp.bfloat16)], axis=0
    )
    my_slots = lax.dynamic_index_in_dim(token_of_slot, exp_index // split_count, 0, keepdims=False)
    picked = normalize(jnp.take(padded, my_slots, axis=0), moe_gain)
    normed_rows = sent([picked], "ctx", 7, True)[0].reshape(ctx_count * CAP, width)
    gate_val = jnp.dot(normed_rows, gate_weight[0], preferred_element_type=jnp.float32)
    up_val = jnp.dot(normed_rows, up_weight[0], preferred_element_type=jnp.float32)
    hidden = (jax.nn.silu(gate_val) * up_val).astype(jnp.bfloat16)
    terms = jnp.dot(hidden, down_weight[0], preferred_element_type=jnp.float32).astype(
        jnp.bfloat16
    )
    arrived_terms = sent([terms.reshape(ctx_count, CAP, width)], "ctx", 8, False)[0]
    sums_mine = jnp.sum(arrived_terms.astype(jnp.float32), axis=0).astype(jnp.bfloat16)
    arrived = lax.all_to_all(sums_mine, "exp", split_axis=1, concat_axis=0, tiled=True)
    piece_expert = jnp.arange(exp_count, dtype=jnp.int32) // split_count
    slot_range = jnp.arange(CAP, dtype=jnp.int32)
    moe_slice = jnp.zeros((tok_rows, slice_width), jnp.float32)
    for k in range(expert_ids.shape[1]):
        hit_expert = expert_ids[:, k, None] == piece_expert[None, :]
        hit_slot = pick_rank[:, k, None] == slot_range[None, :]
        hits = (hit_expert[:, :, None] & hit_slot[:, None, :]).astype(jnp.bfloat16)
        picked_out = jnp.dot(
            hits.reshape(tok_rows, exp_count * CAP), arrived, preferred_element_type=jnp.float32
        )
        moe_slice = moe_slice + route_weight[:, k, None] * picked_out
    return (stream_slice.astype(jnp.float32) + moe_slice).astype(jnp.bfloat16)


def solution(mesh):
    placed = (
        P("ctx", None),
        P("ctx", "exp"),
        P("ctx", "exp"),
        P("ctx", None),
        P("ctx", None),
        P("exp", "ctx"),
        P("exp"),
        P("exp"),
        P("exp"),
        P("exp", "ctx"),
        P(),
        P("exp", None, "ctx"),
        P("exp", None, "ctx"),
        P("exp", "ctx", None),
        P("ctx", None),
        P("ctx", None),
    )
    return jax.shard_map(
        body, mesh=mesh, in_specs=placed, out_specs=P("ctx", "exp"), check_vma=False
    )
```

```python
import functools
import math

import jax
import jax.numpy as jnp
from jax import lax
from jax.experimental import pallas as pl
from jax.experimental.pallas import tpu as pltpu
from jax.sharding import PartitionSpec as P

SPAN = 128
NORM_GROUP = 512
EXPERTS = 8
CAP = 64


EPSILON = 1e-05


MESH = pl.DeviceIdType.MESH


def send_kernel(axis, count, pair, spread, n_arrays, *refs):
    sources, targets = refs[:n_arrays], refs[n_arrays : 2 * n_arrays]
    local_sem, send_sem, recv_sem = refs[2 * n_arrays :]
    index = lax.axis_index(axis)
    group, lane = index // pair, lax.rem(index, pair)
    barrier = pltpu.get_barrier_semaphore()
    peers = [lax.rem(group + d, count) for d in range(1, count)]
    for peer in peers:
        pl.semaphore_signal(
            barrier, inc=1, device_id={axis: peer * pair + lane}, device_id_type=MESH
        )
    pl.semaphore_wait(barrier, count - 1)
    copies = []
    for d, peer in enumerate(peers):
        for i in range(n_arrays):
            copy = pltpu.make_async_remote_copy(
                src_ref=sources[i] if spread else sources[i].at[peer],
                dst_ref=targets[i].at[group],
                send_sem=send_sem.at[d, i],
                recv_sem=recv_sem.at[d, i],
                device_id={axis: peer * pair + lane},
                device_id_type=MESH,
            )
            copy.start()
            copies.append(copy)
    for i in range(n_arrays):
        own = pltpu.make_async_copy(
            sources[i] if spread else sources[i].at[group],
            targets[i].at[group],
            local_sem.at[i],
        )
        own.start()
        copies.append(own)
    for copy in copies:
        copy.wait()


def sent(arrays, axis, number, spread, pair=1):
    count = lax.axis_size(axis) // pair
    n_arrays = len(arrays)
    shapes = [
        jax.ShapeDtypeStruct((count,) + a.shape if spread else a.shape, a.dtype) for a in arrays
    ]
    size = sum(math.prod(shape.shape) * shape.dtype.itemsize for shape in shapes)
    return pl.pallas_call(
        functools.partial(send_kernel, axis, count, pair, spread, n_arrays),
        out_shape=shapes,
        in_specs=[pl.BlockSpec(memory_space=pl.ANY)] * n_arrays,
        out_specs=[pl.BlockSpec(memory_space=pl.ANY)] * n_arrays,
        scratch_shapes=[
            pltpu.SemaphoreType.DMA((n_arrays,)),
            pltpu.SemaphoreType.DMA((count - 1, n_arrays)),
            pltpu.SemaphoreType.DMA((count - 1, n_arrays)),
        ],
        compiler_params=pltpu.CompilerParams(collective_id=number, has_side_effects=True),
        cost_estimate=pl.CostEstimate(flops=0, bytes_accessed=2 * size, transcendentals=0),
    )(*arrays)


def gather_pairs_kernel(axis, groups, x_ref, out_ref, local_sem, send_sem, recv_sem, pass_send, pass_recv):
    index = lax.axis_index(axis)
    group, lane = index // 2, lax.rem(index, 2)
    sibling = group * 2 + 1 - lane
    barrier = pltpu.get_barrier_semaphore()
    peers = [lax.rem(group + d, groups) for d in range(1, groups)]
    for peer in [p * 2 + lane for p in peers] + [sibling]:
        pl.semaphore_signal(barrier, inc=1, device_id={axis: peer}, device_id_type=MESH)
    pl.semaphore_wait(barrier, groups)
    copies = []
    for d, peer in enumerate(peers):
        copy = pltpu.make_async_remote_copy(
            src_ref=x_ref,
            dst_ref=out_ref.at[index],
            send_sem=send_sem.at[d],
            recv_sem=recv_sem.at[d],
            device_id={axis: peer * 2 + lane},
            device_id_type=MESH,
        )
        copy.start()
        copies.append(copy)
    own = pltpu.make_async_copy(x_ref, out_ref.at[index], local_sem)
    own.start()
    passed = [
        pltpu.make_async_remote_copy(
            src_ref=x_ref,
            dst_ref=out_ref.at[index],
            send_sem=pass_send.at[0],
            recv_sem=pass_recv.at[0],
            device_id={axis: sibling},
            device_id_type=MESH,
        )
    ]
    passed[0].start()
    for d in range(1, groups):
        copies[d - 1].wait_recv()
        block = lax.rem(group + groups - d, groups) * 2 + lane
        copy = pltpu.make_async_remote_copy(
            src_ref=out_ref.at[block],
            dst_ref=out_ref.at[block],
            send_sem=pass_send.at[d],
            recv_sem=pass_recv.at[d],
            device_id={axis: sibling},
            device_id_type=MESH,
        )
        copy.start()
        passed.append(copy)
    for copy in copies:
        copy.wait_send()
    own.wait()
    for copy in passed:
        copy.wait()


def gather_pairs(x, axis, number):
    count = lax.axis_size(axis)
    return pl.pallas_call(
        functools.partial(gather_pairs_kernel, axis, count // 2),
        out_shape=jax.ShapeDtypeStruct((count,) + x.shape, x.dtype),
        in_specs=[pl.BlockSpec(memory_space=pl.ANY)],
        out_specs=pl.BlockSpec(memory_space=pl.ANY),
        scratch_shapes=[
            pltpu.SemaphoreType.DMA,
            pltpu.SemaphoreType.DMA((count // 2 - 1,)),
            pltpu.SemaphoreType.DMA((count // 2 - 1,)),
            pltpu.SemaphoreType.DMA((count // 2,)),
            pltpu.SemaphoreType.DMA((count // 2,)),
        ],
        compiler_params=pltpu.CompilerParams(collective_id=number, has_side_effects=True),
        cost_estimate=pl.CostEstimate(
            flops=0, bytes_accessed=2 * count * x.size * x.dtype.itemsize, transcendentals=0
        ),
    )(x)


def pair_sum(halves, number):
    lane = lax.rem(lax.axis_index("exp"), 2)
    both = pair_send(halves, number)
    own = lax.dynamic_index_in_dim(halves, lane, 0, keepdims=False)
    return (own.astype(jnp.float32) + both.astype(jnp.float32)).astype(jnp.bfloat16)


def pair_kernel(x_ref, out_ref, send_sem, recv_sem):
    index = lax.axis_index("exp")
    lane = lax.rem(index, 2)
    sibling = index + 1 - 2 * lane
    barrier = pltpu.get_barrier_semaphore()
    pl.semaphore_signal(barrier, inc=1, device_id={"exp": sibling}, device_id_type=MESH)
    pl.semaphore_wait(barrier, 1)
    copy = pltpu.make_async_remote_copy(
        src_ref=x_ref.at[1 - lane],
        dst_ref=out_ref,
        send_sem=send_sem,
        recv_sem=recv_sem,
        device_id={"exp": sibling},
        device_id_type=MESH,
    )
    copy.start()
    copy.wait()


def pair_send(halves, number):
    return pl.pallas_call(
        pair_kernel,
        out_shape=jax.ShapeDtypeStruct(halves.shape[1:], halves.dtype),
        in_specs=[pl.BlockSpec(memory_space=pl.ANY)],
        out_specs=pl.BlockSpec(memory_space=pl.ANY),
        scratch_shapes=[pltpu.SemaphoreType.DMA, pltpu.SemaphoreType.DMA],
        compiler_params=pltpu.CompilerParams(collective_id=number, has_side_effects=True),
        cost_estimate=pl.CostEstimate(
            flops=0, bytes_accessed=halves.size * 2, transcendentals=0
        ),
    )(halves)


def expert_kernel(x_ref, gate_ref, up_ref, down_ref, out_ref, total):
    step = pl.program_id(1)
    gate_val = jnp.dot(x_ref[...], gate_ref[...], preferred_element_type=jnp.float32)
    up_val = jnp.dot(x_ref[...], up_ref[...], preferred_element_type=jnp.float32)
    hidden = (gate_val / (1.0 + jnp.exp(-gate_val)) * up_val).astype(jnp.bfloat16)
    columns = down_ref.shape[1] // 4

    def add(first):
        for c in range(4):
            part = slice(c * columns, (c + 1) * columns)
            term = jnp.dot(hidden, down_ref[:, part], preferred_element_type=jnp.float32)
            total[:, part] = term if first else total[:, part] + term

    pl.when(step == 0)(lambda: add(True))
    pl.when(step > 0)(lambda: add(False))

    @pl.when(step == pl.num_programs(1) - 1)
    def _():
        out_ref[...] = total[...].astype(out_ref.dtype)


def expert_terms(rows, gate, up, down):
    count, width = rows.shape
    units = gate.shape[1]
    block = 256 if units % 256 == 0 else 128
    tall = 256 if count % 256 == 0 else count
    return pl.pallas_call(
        expert_kernel,
        out_shape=jax.ShapeDtypeStruct((count, width), jnp.bfloat16),
        grid=(count // tall, units // block),
        in_specs=[
            pl.BlockSpec((tall, width), lambda r, i: (r, 0)),
            pl.BlockSpec((width, block), lambda r, i: (0, i)),
            pl.BlockSpec((width, block), lambda r, i: (0, i)),
            pl.BlockSpec((block, width), lambda r, i: (i, 0)),
        ],
        out_specs=pl.BlockSpec((tall, width), lambda r, i: (r, 0)),
        scratch_shapes=[pltpu.VMEM((tall, width), jnp.float32)],
        compiler_params=pltpu.CompilerParams(vmem_limit_bytes=48 * 1024 * 1024),
        cost_estimate=pl.CostEstimate(
            flops=6 * count * width * units,
            bytes_accessed=6 * width * units,
            transcendentals=count * units,
        ),
    )(rows, gate, up, down)


def slot_tables(block_ids):
    expert_range = jnp.arange(EXPERTS, dtype=jnp.int32)
    hit_table = jnp.sum(
        (block_ids[:, :, None] == expert_range[None, None, :]).astype(jnp.int32), axis=1
    )
    ranking = jnp.cumsum(hit_table, axis=0) - 1
    slot_range = jnp.arange(CAP, dtype=jnp.int32)
    matches = (hit_table.T[:, None, :] == 1) & (ranking.T[:, None, :] == slot_range[None, :, None])
    row_count = block_ids.shape[0]
    row_range = jnp.arange(row_count, dtype=jnp.int32)
    chosen = jnp.sum(jnp.where(matches, row_range[None, None, :], 0), axis=2)
    filled = jnp.any(matches, axis=2)
    token_of_slot = jnp.where(filled, chosen, row_count)
    pick_rank = jnp.take_along_axis(ranking, block_ids, axis=1)
    return (token_of_slot, pick_rank)


def normalize(stream_rows, moe_gain):
    values = stream_rows.astype(jnp.float32)
    scale_inv = lax.rsqrt(jnp.mean(values * values, axis=-1, keepdims=True) + EPSILON)
    return (values * scale_inv * moe_gain).astype(jnp.bfloat16)


def body(
    residual,
    ssm_input,
    ssm_gate,
    write_vectors,
    read_vectors,
    step_logits,
    decay_log,
    skip_gain,
    norm_gain,
    out_weight,
    moe_gain,
    gate_weight,
    up_weight,
    down_weight,
    expert_ids,
    route_weight,
):
    heads_dev = step_logits.shape[0]
    tok_rows = step_logits.shape[1]
    head_width = ssm_input.shape[1] // heads_dev
    span_count = tok_rows // SPAN
    step_size = jax.nn.softplus(step_logits)
    log_step = step_size * (-jnp.exp(decay_log))[:, None]
    cumulative = jnp.cumsum(log_step.reshape(heads_dev, span_count, SPAN), axis=2)
    step_blocks = step_size.reshape(heads_dev, span_count, SPAN)
    input_blocks = ssm_input.reshape(span_count, SPAN, heads_dev, head_width)
    write_blocks = write_vectors.reshape(span_count, SPAN, -1)
    read_blocks = read_vectors.reshape(span_count, SPAN, -1)
    scores = jnp.einsum(
        "ktn,ksn->kts", read_blocks, write_blocks, preferred_element_type=jnp.float32
    )
    causal = jnp.arange(SPAN)[:, None] >= jnp.arange(SPAN)[None, :]
    log_gaps = cumulative[:, :, :, None] - cumulative[:, :, None, :]
    mixing = jnp.where(
        causal,
        scores[None] * jnp.exp(jnp.where(causal, log_gaps, 0.0)) * step_blocks[:, :, None, :],
        0.0,
    ).astype(jnp.bfloat16)
    intra_out = jnp.einsum(
        "hkts,kshp->kthp", mixing, input_blocks, preferred_element_type=jnp.float32
    )
    end_weight = jnp.exp(cumulative[:, :, -1:] - cumulative) * step_blocks
    loaded = (end_weight[:, :, :, None] * write_blocks.astype(jnp.float32)[None]).astype(
        jnp.bfloat16
    )
    block_state = jnp.einsum(
        "kshp,hksn->hkpn", input_blocks, loaded, preferred_element_type=jnp.float32
    )
    block_decay = jnp.exp(cumulative[:, :, -1])
    running = jnp.zeros_like(block_state[:, 0])
    decay_run = jnp.ones_like(block_decay[:, 0])
    entering_list = [running]
    reach_list = [decay_run]
    running = block_decay[:, 0, None, None] * running + block_state[:, 0]
    decay_run = decay_run * block_decay[:, 0]
    device_state = running
    device_decay = decay_run

    all_states, all_decays = sent(
        [
            device_state.astype(jnp.bfloat16),
            jnp.broadcast_to(device_decay[:, None], (heads_dev, 128)),
        ],
        "ctx",
        1,
        True,
    )
    ctx_index = lax.axis_index("ctx")
    device_in = jnp.zeros_like(device_state)
    for j in range(lax.axis_size("ctx") - 1):
        device_in = jnp.where(
            j < ctx_index,
            all_decays[j, :, :1, None] * device_in + all_states[j].astype(jnp.float32),
            device_in,
        )
    entering = jnp.stack(entering_list, axis=1)
    reach = jnp.stack(reach_list, axis=1)
    states = entering + reach[:, :, None, None] * device_in[:, None]
    inter_out = jnp.transpose(jnp.exp(cumulative), (1, 2, 0))[:, :, :, None] * jnp.einsum(
        "ktn,hkpn->kthp", read_blocks.astype(jnp.float32), states, precision=lax.Precision.HIGHEST
    )
    scan_out = (
        intra_out + inter_out + skip_gain[None, None, :, None] * input_blocks.astype(jnp.float32)
    )
    scan_out = scan_out.reshape(tok_rows, heads_dev * head_width)
    gated_out = scan_out * jax.nn.silu(ssm_gate.astype(jnp.float32))
    grouped = gated_out.reshape(tok_rows, -1, NORM_GROUP)
    group_scale = lax.rsqrt(jnp.mean(grouped * grouped, axis=2, keepdims=True) + EPSILON)
    normed = ((grouped * group_scale).reshape(tok_rows, -1) * norm_gain).astype(jnp.bfloat16)
    ctx_count = lax.axis_size("ctx")
    exp_count = lax.axis_size("exp")
    exp_index = lax.axis_index("exp")
    width = residual.shape[1]
    slice_width = width // exp_count
    split_count = exp_count // EXPERTS
    own_rows = tok_rows // exp_count
    normed_all = sent([normed], "ctx", 2, True)[0].reshape(ctx_count * tok_rows, -1)
    ssm_terms = jnp.dot(normed_all, out_weight, preferred_element_type=jnp.float32).astype(
        jnp.bfloat16
    )
    groups = exp_count // 2
    by_owner = jnp.transpose(
        ssm_terms.reshape(ctx_count, groups, 2, own_rows, -1), (2, 1, 0, 3, 4)
    ).reshape(2, groups * ctx_count * own_rows, -1)
    halves = pair_sum(by_owner, 3)
    chips = sent([halves.reshape(groups, ctx_count * own_rows, -1)], "exp", 4, False, 2)[0]
    ssm_part = jnp.sum(chips.astype(jnp.float32), axis=0).astype(jnp.bfloat16)
    ssm_rows = sent([ssm_part.reshape(ctx_count, own_rows, -1)], "ctx", 5, False)[0]
    ssm_rows = jnp.transpose(ssm_rows, (1, 0, 2)).reshape(own_rows, width)
    own_residual = lax.dynamic_slice_in_dim(residual, exp_index * own_rows, own_rows, 0)
    stream_rows = (own_residual.astype(jnp.float32) + ssm_rows.astype(jnp.float32)).astype(
        jnp.bfloat16
    )
    token_of_slot, pick_rank = slot_tables(expert_ids)
    stream_full = gather_pairs(stream_rows, "exp", 6).reshape(tok_rows, width)
    stream_slice = lax.dynamic_slice_in_dim(stream_full, exp_index * slice_width, slice_width, 1)
    padded = jnp.concatenate(
        [stream_full, jnp.zeros((1, stream_full.shape[1]), jnp.bfloat16)], axis=0
    )
    my_slots = lax.dynamic_index_in_dim(token_of_slot, exp_index // split_count, 0, keepdims=False)
    picked = normalize(jnp.take(padded, my_slots, axis=0), moe_gain)
    normed_rows = sent([picked], "ctx", 7, True)[0].reshape(ctx_count * CAP, width)
    terms = expert_terms(normed_rows, gate_weight[0], up_weight[0], down_weight[0])
    arrived_terms = sent([terms.reshape(ctx_count, CAP, width)], "ctx", 8, False)[0]
    sums_mine = jnp.sum(arrived_terms.astype(jnp.float32), axis=0).astype(jnp.bfloat16)
    by_slice = jnp.transpose(sums_mine.reshape(CAP, exp_count, slice_width), (1, 0, 2))
    arrived = sent([by_slice], "exp", 9, False)[0].reshape(exp_count * CAP, slice_width)
    piece_expert = jnp.arange(exp_count, dtype=jnp.int32) // split_count
    slot_range = jnp.arange(CAP, dtype=jnp.int32)
    moe_slice = jnp.zeros((tok_rows, slice_width), jnp.float32)
    for k in range(expert_ids.shape[1]):
        hit_expert = expert_ids[:, k, None] == piece_expert[None, :]
        hit_slot = pick_rank[:, k, None] == slot_range[None, :]
        hits = (hit_expert[:, :, None] & hit_slot[:, None, :]).astype(jnp.bfloat16)
        picked_out = jnp.dot(
            hits.reshape(tok_rows, exp_count * CAP), arrived, preferred_element_type=jnp.float32
        )
        moe_slice = moe_slice + route_weight[:, k, None] * picked_out
    return (stream_slice.astype(jnp.float32) + moe_slice).astype(jnp.bfloat16)


def solution(mesh):
    placed = (
        P("ctx", None),
        P("ctx", "exp"),
        P("ctx", "exp"),
        P("ctx", None),
        P("ctx", None),
        P("exp", "ctx"),
        P("exp"),
        P("exp"),
        P("exp"),
        P("exp", "ctx"),
        P(),
        P("exp", None, "ctx"),
        P("exp", None, "ctx"),
        P("exp", "ctx", None),
        P("ctx", None),
        P("ctx", None),
    )
    return jax.shard_map(
        body, mesh=mesh, in_specs=placed, out_specs=P("ctx", "exp"), check_vma=False
    )
```
